512 devices in a mesh: section: 8 (over z), expert: 64 (over y, x, core).
Axes of the slice: x: 4, y: 8, z: 8, core: 2. Of those that a mesh axis runs over, the one named last changes fastest.
Arguments:
- feat_saved: bfloat16 [8, 2, 8192, 1024], P('section', None, 'expert'), may hold values from -6 to 6
- out_grad: bfloat16 [2, 8192, 1024], P(None, 'expert'), may hold values from -6 to 6
- lengths: int32 [2, 64], P(None, 'expert'), may hold values from 32 to 128, as said below
- expert_ids: int32 [8, 2, 8192], P('section', None, 'expert'), may hold values from 0 to 63, as said below
- slot_ids: int32 [8, 2, 8192], P('section', None, 'expert'), may hold values from 0 to 2, as said below
- expert_preact: bfloat16 [8, 2, 12288, 640], P('section', None, 'expert'), may hold values from -6 to 6
- conv_weight: bfloat16 [8, 32, 1024], P('section'), may hold values from -0.5 to 0.5
- norm_gain: bfloat16 [8, 1024], P('section'), may hold values from 0.5 to 1.5
- centroids: bfloat16 [8, 64, 1024], P('section'), may hold values from -0.375 to 0.375
- w_in: bfloat16 [8, 64, 1024, 640], P('section', 'expert'), may hold values from -0.1875 to 0.1875
- w_out: bfloat16 [8, 64, 640, 1024], P('section', 'expert'), may hold values from -0.25 to 0.25
Outputs:
- section_grads: bfloat16 [8, 2, 8192, 1024], P('section', None, 'expert')
The draws below stay inside these ranges and needn't reach their ends.
Inputs may be any that keep to these rules, and one draw needn't show every extreme that they name: `expert_ids`: in every block and micro-batch, the 128 frames of one utterance name each expert at most 3 times, and one expert is named exactly 3 times by the frames of every utterance. `slot_ids`: within one utterance's frames of one block and micro-batch, the frames that name the same expert hold the slots 0, 1, ... up to their count less one, each once. `lengths`: in every micro-batch at least one utterance has all 128 frames.
All inputs are finite; a program needn't handle non-finite values.
Results may differ from the reference program's by a relative error of at most 0.02.
Values may be sent and summed in bfloat16 or wider, within the bound.
No kernel may reach another device: no remote copies, remote signals or barrier semaphores. Data moves between devices by JAX's collectives and lax.ppermute only.
A program may use at most 64 MiB of HBM per device.

```python
import math
import jax
import jax.numpy as jnp
from jax import lax

D = 1024
HID = 640
KER = 32
FRAMES_DEV = 128
MICRO = 2
SECTIONS = 8
EXPERTS = 64
UTTS = 64
FRAMES = 8192
CAP = 3
SLOTS = 192


def routing_tables(key):
    candidates = EXPERTS * CAP
    hot_expert = jax.random.randint(jax.random.fold_in(key, 11), (SECTIONS, MICRO, 1, 1, 1), 0, EXPERTS)
    table_shape = (SECTIONS, MICRO, EXPERTS, EXPERTS, 1)
    strides = jax.random.randint(jax.random.fold_in(key, 12), table_shape, 3, 13)
    offsets = jax.random.randint(jax.random.fold_in(key, 13), table_shape, 0, 4)
    expert_idx = jnp.arange(EXPERTS).astype(jnp.int32).reshape(1, 1, 1, EXPERTS, 1)
    slot_idx = jnp.arange(CAP).astype(jnp.int32).reshape(1, 1, 1, 1, CAP)
    is_hot = expert_idx == hot_expert
    strides = jnp.where(is_hot, 1, strides)
    offsets = jnp.where(is_hot, 0, offsets)
    order_key = slot_idx * strides + offsets
    rank_val = (expert_idx - hot_expert) % EXPERTS * CAP + slot_idx
    scores = (order_key * candidates + rank_val).reshape(SECTIONS, MICRO, EXPERTS, candidates)
    chosen_neg, chosen = lax.top_k(-scores, FRAMES_DEV)
    chosen_expert = chosen // CAP
    chosen_slot = chosen % CAP
    shuffle_raw = jax.random.randint(jax.random.fold_in(key, 14), (SECTIONS, MICRO, EXPERTS, FRAMES_DEV), 0, 2 ** 20) * FRAMES_DEV + jnp.arange(FRAMES_DEV).astype(jnp.int32)
    shuffle_val, shuffle = lax.top_k(shuffle_raw, FRAMES_DEV)
    routed = jnp.take_along_axis(chosen_expert, shuffle, axis=3).reshape(SECTIONS, MICRO, EXPERTS * FRAMES_DEV)
    slot_rows = jnp.take_along_axis(chosen_slot, shuffle, axis=3).reshape(SECTIONS, MICRO, EXPERTS * FRAMES_DEV)
    return (routed.astype(jnp.int32), slot_rows.astype(jnp.int32))


def draw_expert_ids(key, part):
    return routing_tables(key)[0]


def draw_slot_ids(key, part):
    return routing_tables(key)[1]


def draw_lengths(key, part):
    base_len = jax.random.randint(jax.random.fold_in(key, 21), (MICRO, UTTS), FRAMES_DEV // 4, FRAMES_DEV + 1)
    full_utt = jax.random.randint(jax.random.fold_in(key, 22), (MICRO, 1), 0, UTTS)
    utt_idx = jnp.arange(UTTS).astype(jnp.int32)[None, :]
    return jnp.where(utt_idx == full_utt, FRAMES_DEV, base_len).astype(jnp.int32)


def levels(rng, shape, shards, least, top_value):
    def one(axis_at, parts):
        heights = jax.random.uniform(jax.random.fold_in(jax.random.fold_in(rng, 6), axis_at), (parts,), jnp.float32, least / len(shards), top_value / len(shards))
        return jnp.repeat(jnp.exp(heights), shape[axis_at] // parts).reshape((-1,) + (1,) * (len(shape) - axis_at - 1))

    gain = one(*shards[0])
    for cut in shards[1:]:
        gain = gain * one(*cut)
    return gain


def noise(stream_key, extent, width, limit, cuts=(), held_as=jnp.bfloat16):
    level = levels(stream_key, extent, cuts, -0.22, 0.18) if cuts else 1.0
    entries = jax.random.normal(stream_key, extent, jnp.float32) * width * level
    return jnp.minimum(jnp.maximum(entries, -limit), limit).astype(held_as)


def setup_inputs(seed: int = 0) -> dict:
    splits = jax.random.split(jax.random.key(seed), 12)
    feat_saved = noise(splits[0], (SECTIONS, MICRO, FRAMES, D), 1.0, 6.0, ((0, 8), (2, 64)))
    out_grad = noise(splits[1], (MICRO, FRAMES, D), 1.0, 6.0, ((1, 64),))
    lengths = draw_lengths(jax.random.fold_in(splits[11], 71), 0)
    expert_ids = draw_expert_ids(jax.random.fold_in(splits[11], 71), 0)
    slot_ids = draw_slot_ids(jax.random.fold_in(splits[11], 71), 0)
    expert_preact = noise(splits[5], (SECTIONS, MICRO, EXPERTS * SLOTS, HID), 1.0, 6.0, ((0, 8), (2, 64)))
    conv_weight = noise(splits[6], (SECTIONS, KER, D), (4 * KER) ** -0.5, 0.5, ((0, 8),))
    norm_gain = jnp.clip(1.0 + 0.1 * jax.random.normal(splits[7], (SECTIONS, D), jnp.float32), 0.5, 1.5).astype(jnp.bfloat16)
    centroids = noise(splits[8], (SECTIONS, EXPERTS, D), (D // 4) ** -0.5, 0.375, ((0, 8),))
    w_in = noise(splits[9], (SECTIONS, EXPERTS, D, HID), D ** -0.5, 0.1875, ((0, 8), (1, 64)))
    w_out = noise(splits[10], (SECTIONS, EXPERTS, HID, D), HID ** -0.5, 0.25, ((0, 8), (1, 64)))
    return {"feat_saved": feat_saved, "out_grad": out_grad, "lengths": lengths, "expert_ids": expert_ids, "slot_ids": slot_ids, "expert_preact": expert_preact, "conv_weight": conv_weight, "norm_gain": norm_gain, "centroids": centroids, "w_in": w_in, "w_out": w_out}


def time_conv(values, kernel, low_pad):
    tap_count = kernel.shape[0]
    frames = values.shape[-2]
    widths = [(0, 0)] * (values.ndim - 2) + [(low_pad, tap_count - 1 - low_pad), (0, 0)]
    padded = jnp.pad(values, widths)
    summed = jnp.zeros_like(values)
    for tap_idx in range(tap_count):
        summed = summed + kernel[tap_idx] * lax.slice_in_dim(padded, tap_idx, tap_idx + frames, axis=values.ndim - 2)
    return summed

def gelu_parts(preact):
    act_val = preact.astype(jnp.float32)
    cdf_val = 0.5 * (1.0 + jax.scipy.special.erf(act_val * (1.0 / math.sqrt(2.0))))
    gelu_val = act_val * cdf_val
    gelu_slope = cdf_val + act_val * jnp.exp(-0.5 * act_val * act_val) * (1.0 / math.sqrt(2.0 * math.pi))
    return (gelu_val, gelu_slope)

def expert_back(operands):
    slot_rows, preact, weight_in, weight_out = operands
    hidden_grad = lax.dot_general(slot_rows, weight_out, (((1,), (1,)), ((), ())), preferred_element_type=jnp.float32)
    gelu_val, gelu_slope = gelu_parts(preact)
    gate_grad = lax.optimization_barrier(jnp.sum(hidden_grad * gelu_val, axis=1))
    pre_grad = (hidden_grad * gelu_slope).astype(jnp.bfloat16)
    slot_grad = lax.dot_general(pre_grad, weight_in, (((1,), (1,)), ((), ())), preferred_element_type=jnp.float32)
    return (slot_grad.astype(jnp.bfloat16), gate_grad)

def block_ref(grad_in, feats, frame_mask, routed, slot_pos, preact, conv_k, gain_vec, cent_table, weight_in, weight_out, source):
    conv_f = conv_k.astype(jnp.float32)
    gain_f = gain_vec.astype(jnp.float32)
    feats3 = feats.astype(jnp.float32).reshape(UTTS, FRAMES_DEV, D)
    pre_act = time_conv(feats3 * frame_mask, conv_f, KER // 2)
    sig_pre = jax.nn.sigmoid(pre_act)
    residual = (feats3 + frame_mask * pre_act * sig_pre).reshape(FRAMES, D)
    inv_rms = lax.rsqrt(lax.optimization_barrier(jnp.mean(residual * residual, axis=1, keepdims=True)) + 1e-06)
    normed = (residual * inv_rms * gain_f).astype(jnp.bfloat16)
    score_all = jnp.dot(normed, cent_table.T, preferred_element_type=jnp.float32)
    score_val = jnp.take_along_axis(score_all, routed[:, None], axis=1)[:, 0]
    gate_val = jax.nn.sigmoid(score_val)
    cent_rows = cent_table[routed].astype(jnp.float32)
    position = (routed * SLOTS + source * CAP + slot_pos).astype(jnp.int32)
    bucket = jnp.zeros((EXPERTS * SLOTS, D), jnp.bfloat16).at[position].set(grad_in)
    grads_all, gates_all = lax.map(expert_back, (bucket.reshape(EXPERTS, SLOTS, D), preact.reshape(EXPERTS, SLOTS, HID), weight_in, weight_out))
    slot_grad = grads_all.reshape(EXPERTS * SLOTS, D)[position].astype(jnp.float32)
    gate_grad = gates_all.reshape(EXPERTS * SLOTS)[position]
    total_grad = gate_val[:, None] * slot_grad + (gate_val * (1.0 - gate_val) * gate_grad)[:, None] * cent_rows
    scaled = total_grad * gain_f
    cubed = inv_rms * inv_rms * inv_rms
    resid_grad = grad_in.astype(jnp.float32) + inv_rms * scaled - residual * cubed * lax.optimization_barrier(jnp.mean(residual * scaled, axis=1, keepdims=True))
    resid3 = resid_grad.reshape(UTTS, FRAMES_DEV, D)
    conv_slope = frame_mask * sig_pre * (1.0 + pre_act * (1.0 - sig_pre))
    conv_back = time_conv(conv_slope * resid3, conv_f[::-1], KER - 1 - KER // 2)
    return (resid3 + frame_mask * conv_back).reshape(FRAMES, D).astype(jnp.bfloat16)

def reference(feat_saved, out_grad, lengths, expert_ids, slot_ids, expert_preact, conv_weight, norm_gain, centroids, w_in, w_out):
    frame_pos = jnp.arange(FRAMES_DEV).astype(jnp.int32)
    source = (jnp.arange(FRAMES) // FRAMES_DEV).astype(jnp.int32)
    results = [[None] * MICRO for section_idx in range(SECTIONS)]
    for micro_idx in range(MICRO):
        frame_mask = (frame_pos[None, :] < lengths[micro_idx][:, None]).astype(jnp.float32)[:, :, None]
        grad_now = out_grad[micro_idx]
        for section_idx in reversed(range(SECTIONS)):
            grad_now = block_ref(grad_now, feat_saved[section_idx, micro_idx], frame_mask, expert_ids[section_idx, micro_idx], slot_ids[section_idx, micro_idx], expert_preact[section_idx, micro_idx], conv_weight[section_idx], norm_gain[section_idx], centroids[section_idx], w_in[section_idx], w_out[section_idx], source)
            results[section_idx][micro_idx] = grad_now
    return jnp.stack([jnp.stack(section_row) for section_row in results])
```

```python
import functools
import math

import jax
import jax.numpy as jnp
from jax import lax
from jax.experimental import pallas as pl
from jax.experimental.pallas import tpu as pltpu
from jax.sharding import PartitionSpec as P

SUB = 8
LANES = 128
BLOCK = 8
F32 = jnp.float32
BF16 = jnp.bfloat16


def gelu_parts(preact):
    act_val = preact.astype(F32)
    cdf_val = 0.5 * (1.0 + lax.erf(act_val * (1.0 / math.sqrt(2.0))))
    gelu_val = act_val * cdf_val
    gelu_slope = cdf_val + act_val * jnp.exp(-0.5 * act_val * act_val) * (
        1.0 / math.sqrt(2.0 * math.pi)
    )
    return gelu_val, gelu_slope


def tiles(array):
    return array.reshape(array.shape[:-1] + (SUB, array.shape[-1] // SUB))


def conv_block(src_ref, taps_ref, base, reverse):
    count = taps_ref.shape[0]
    acc = [None] * BLOCK
    for j in range(BLOCK + count - 1):
        at = j + 1 if reverse else j
        row = src_ref[base + at]
        for i in range(BLOCK):
            k = i + count - at if reverse else at - i
            if 0 <= k < count:
                term = taps_ref[k] * row
                acc[i] = term if acc[i] is None else acc[i] + term
    return acc


def tile_sum(array):
    return jnp.sum(jnp.sum(array, axis=1, keepdims=True), axis=2, keepdims=True)


def prep_kernel(
    cap,
    len_ref,
    ids_ref,
    row_ref,
    info_row_ref,
    feat_ref,
    grad_ref,
    taps_ref,
    gain_ref,
    cent_ref,
    normed_ref,
    slope_ref,
    pay_ref,
    padded,
    info,
):
    micros, frames = ids_ref.shape
    half = taps_ref.shape[0] // 2
    experts = cent_ref.shape[0]
    per_expert = pay_ref.shape[0] // experts
    info_tiles = per_expert - micros * cap
    channels = feat_ref.shape[2] * feat_ref.shape[3]
    gain = gain_ref[...][None]
    pay_ref[...] = jnp.zeros_like(pay_ref)
    info[...] = jnp.zeros_like(info)
    edge = jnp.zeros((half,) + padded.shape[1:], F32)
    padded[pl.ds(0, half)] = edge
    padded[pl.ds(half + frames, half)] = edge
    lane = lax.broadcasted_iota(jnp.int32, (1, LANES), 1)

    for m in range(micros):
        length = len_ref[m]

        def fill(block, _):
            base = block * BLOCK
            time = base + lax.broadcasted_iota(jnp.int32, (BLOCK, SUB, LANES), 0)
            rows = feat_ref[m, pl.ds(base, BLOCK)].astype(F32)
            padded[pl.ds(half + base, BLOCK)] = jnp.where(time < length, rows, 0.0)
            return 0

        lax.fori_loop(0, frames // BLOCK, fill, 0)

        def step(block, _):
            base = block * BLOCK
            time = base + lax.broadcasted_iota(jnp.int32, (BLOCK, SUB, LANES), 0)
            mask = (time < length).astype(F32)
            pre = jnp.stack(conv_block(padded, taps_ref, base, False))
            sig = 1.0 / (1.0 + jnp.exp(-pre))
            residual = feat_ref[m, pl.ds(base, BLOCK)].astype(F32) + mask * pre * sig
            inv = lax.rsqrt(tile_sum(residual * residual) * (1.0 / channels) + 1e-6)
            scaled = residual * inv
            normed_ref[m, pl.ds(base, BLOCK)] = scaled.astype(BF16)
            slope_ref[m, pl.ds(base, BLOCK)] = (
                mask * sig * (1.0 + pre * (1.0 - sig))
            ).astype(BF16)
            normed = (scaled * gain).astype(BF16).astype(F32)
            cents = jnp.stack(
                [cent_ref[ids_ref[m, base + i]].astype(F32) for i in range(BLOCK)]
            )
            gate = 1.0 / (1.0 + jnp.exp(-tile_sum(normed * cents)))
            first = inv * gate
            second = first * (1.0 - gate)
            first_hi = first.astype(BF16).astype(F32)
            second_hi = second.astype(BF16).astype(F32)
            for i in range(BLOCK):
                line = jnp.where(lane == 0, first_hi[i], 0.0)
                line = jnp.where(lane == 1, first[i] - first_hi[i], line)
                line = jnp.where(lane == 2, second_hi[i], line)
                line = jnp.where(lane == 3, second[i] - second_hi[i], line)
                info[pl.ds(info_row_ref[m, base + i], 1), :] = line
                pay_ref[row_ref[m, base + i]] = grad_ref[m, base + i]
            return 0

        lax.fori_loop(0, frames // BLOCK, step, 0)

    def put_info(expert, _):
        for t in range(info_tiles):
            rows = info[pl.ds(pl.multiple_of((expert * info_tiles + t) * SUB, SUB), SUB), :]
            pay_ref[expert * per_expert + micros * cap + t] = rows.astype(BF16)
        return 0

    lax.fori_loop(0, experts, put_info, 0)


def prep(lengths, ids, slots, feats, grads, taps, gain, cents, cap):
    micros, frames = ids.shape
    experts = cents.shape[0]
    info_tiles = -(-micros * cap // SUB)
    per_expert = micros * cap + info_tiles
    which = lax.iota(jnp.int32, micros)[:, None] * cap + slots
    smem = pl.BlockSpec(memory_space=pltpu.SMEM)
    vmem = pl.BlockSpec(memory_space=pltpu.VMEM)
    normed, slope, payload = pl.pallas_call(
        functools.partial(prep_kernel, cap),
        out_shape=(
            jax.ShapeDtypeStruct(feats.shape, BF16),
            jax.ShapeDtypeStruct(feats.shape, BF16),
            jax.ShapeDtypeStruct((experts * per_expert, SUB, LANES), BF16),
        ),
        in_specs=[smem] * 4 + [vmem] * 5,
        out_specs=[vmem] * 3,
        scratch_shapes=[
            pltpu.VMEM((frames + taps.shape[0], SUB, LANES), F32),
            pltpu.VMEM((experts * info_tiles * SUB, LANES), F32),
        ],
        name="prep",
    )(
        lengths,
        ids,
        ids * per_expert + which,
        ids * (info_tiles * SUB) + which,
        feats,
        grads,
        taps,
        gain,
        cents,
    )
    return normed, slope, payload.reshape(experts, per_expert * SUB, LANES)


def expert_kernel(
    rows_ref,
    gate_ref,
    gelu_ref,
    slope_ref,
    w_out_ref,
    w_in_ref,
    cent_ref,
    gain_ref,
    out_ref,
    wide,
    left,
    total,
    gates,
):
    chunk = pl.program_id(1)
    slots = left.shape[0]

    @pl.when(chunk == 0)
    def _():
        wide[...] = rows_ref[...].reshape(wide.shape).astype(F32)
        for q in range(SUB):
            left[:, q * LANES : (q + 1) * LANES] = wide[pl.ds(q, slots, stride=SUB), :].astype(BF16)

    dims = (((1,), (1,)), ((), ()))
    gate = gate_ref[0].astype(F32)
    first = gate[:, 0:1] + gate[:, 1:2]
    hidden = lax.dot_general(left[...], w_out_ref[...], dims, preferred_element_type=F32)
    pre_grad = (hidden * slope_ref[0].astype(F32) * first).astype(BF16)
    part = lax.dot_general(pre_grad, w_in_ref[...], dims, preferred_element_type=F32)
    gated = hidden * gelu_ref[0].astype(F32)

    @pl.when(chunk == 0)
    def _():
        total[...] = part
        gates[...] = gated

    @pl.when(chunk > 0)
    def _():
        total[...] += part
        gates[...] += gated

    @pl.when(chunk == pl.num_programs(1) - 1)
    def _():
        second = gate[:, 2:3] + gate[:, 3:4]
        weight = second * jnp.sum(gates[...], axis=1, keepdims=True)
        for q in range(SUB):
            cols = slice(q * LANES, (q + 1) * LANES)
            wide[pl.ds(q, slots, stride=SUB), :] = (
                total[:, cols] + weight * cent_ref[:, cols]
            ) * gain_ref[:, cols]
        out_ref[...] = wide[...].astype(BF16).reshape(out_ref.shape)


def expert(rows, gate, gelu, slope, w_out, w_in, cent, gain):
    micros, slots, hidden = gelu.shape
    devices = rows.shape[0]
    cap = slots // devices
    width = w_in.shape[0]
    chunk = LANES
    block = (devices, cap, SUB, LANES)
    whole = pl.BlockSpec((1, width), lambda m, c: (0, 0))
    return pl.pallas_call(
        expert_kernel,
        grid=(micros, hidden // chunk),
        out_shape=jax.ShapeDtypeStruct((devices, micros * cap, SUB, LANES), BF16),
        in_specs=[
            pl.BlockSpec(block, lambda m, c: (0, m, 0, 0)),
            pl.BlockSpec((1, slots, LANES), lambda m, c: (m, 0, 0)),
            pl.BlockSpec((1, slots, chunk), lambda m, c: (m, 0, c)),
            pl.BlockSpec((1, slots, chunk), lambda m, c: (m, 0, c)),
            pl.BlockSpec((chunk, width), lambda m, c: (c, 0)),
            pl.BlockSpec((width, chunk), lambda m, c: (0, c)),
            whole,
            whole,
        ],
        out_specs=pl.BlockSpec(block, lambda m, c: (0, m, 0, 0)),
        scratch_shapes=[
            pltpu.VMEM((slots * SUB, LANES), F32),
            pltpu.VMEM((slots, width), BF16),
            pltpu.VMEM((slots, width), F32),
            pltpu.VMEM((slots, chunk), F32),
        ],
        name="expert",
    )(rows, gate, gelu, slope, w_out, w_in, cent, gain)


def frame_kernel(
    len_ref, row_ref, back_ref, grad_ref, normed_ref, slope_ref, taps_ref, out_ref, held, padded
):
    m = pl.program_id(0)
    frames = grad_ref.shape[1]
    half = taps_ref.shape[0] // 2
    channels = grad_ref.shape[2] * grad_ref.shape[3]
    length = len_ref[m]
    edge = jnp.zeros((half,) + padded.shape[1:], F32)
    padded[pl.ds(0, half)] = edge
    padded[pl.ds(half + frames, half)] = edge

    def norm(block, _):
        base = block * BLOCK
        back = jnp.stack([back_ref[row_ref[m, base + i]].astype(F32) for i in range(BLOCK)])
        normed = normed_ref[0, pl.ds(base, BLOCK)].astype(F32)
        mean = tile_sum(normed * back) * (1.0 / channels)
        resid = grad_ref[0, pl.ds(base, BLOCK)].astype(F32) + back - normed * mean
        held[pl.ds(base, BLOCK)] = resid
        padded[pl.ds(half + base, BLOCK)] = resid * slope_ref[0, pl.ds(base, BLOCK)].astype(F32)
        return 0

    lax.fori_loop(0, frames // BLOCK, norm, 0)

    def conv(block, _):
        base = block * BLOCK
        time = base + lax.broadcasted_iota(jnp.int32, (BLOCK, SUB, LANES), 0)
        summed = jnp.stack(conv_block(padded, taps_ref, base, True))
        resid = held[pl.ds(base, BLOCK)]
        out_ref[0, pl.ds(base, BLOCK)] = jnp.where(time < length, resid + summed, resid).astype(
            BF16
        )
        return 0

    lax.fori_loop(0, frames // BLOCK, conv, 0)


def frame(lengths, rows, back, grads, normed, slope, taps):
    micros, frames = rows.shape
    smem = pl.BlockSpec(memory_space=pltpu.SMEM)
    block = pl.BlockSpec((1,) + grads.shape[1:], lambda m: (m, 0, 0, 0))
    whole = lambda array: pl.BlockSpec(array.shape, lambda m: (0, 0, 0))
    return pl.pallas_call(
        frame_kernel,
        grid=(micros,),
        out_shape=jax.ShapeDtypeStruct(grads.shape, BF16),
        in_specs=[smem, smem, whole(back), block, block, block, whole(taps)],
        out_specs=block,
        scratch_shapes=[
            pltpu.VMEM((frames, SUB, LANES), F32),
            pltpu.VMEM((frames + taps.shape[0], SUB, LANES), F32),
        ],
        name="frame",
    )(lengths, rows, back, grads, normed, slope, taps)


def bucket_kernel(take_ref, row_ref, kept_ref, came_ref, bucket_ref, grad_ref):
    frames = kept_ref.shape[0]
    bucket_ref[...] = jnp.zeros_like(bucket_ref)

    def move(source):
        def step(block, _):
            base = block * BLOCK
            for i in range(BLOCK):
                row = source[base + i]
                grad_ref[base + i] = row
                bucket_ref[row_ref[base + i]] = row
            return 0

        lax.fori_loop(0, frames // BLOCK, step, 0)

    @pl.when(take_ref[0] != 0)
    def _():
        move(came_ref)

    @pl.when(take_ref[0] == 0)
    def _():
        move(kept_ref)


def bucket(take, rows, kept, came, slots):
    smem = pl.BlockSpec(memory_space=pltpu.SMEM)
    vmem = pl.BlockSpec(memory_space=pltpu.VMEM)
    return pl.pallas_call(
        bucket_kernel,
        out_shape=(
            jax.ShapeDtypeStruct((slots, SUB, LANES), BF16),
            jax.ShapeDtypeStruct(kept.shape, BF16),
        ),
        in_specs=[smem, smem, vmem, vmem],
        out_specs=[vmem, vmem],
        name="bucket",
    )(take, rows, kept, came)


def exchange(array):
    return lax.all_to_all(array, "expert", split_axis=0, concat_axis=0, tiled=True)


def on_device(
    feat_saved,
    out_grad,
    lengths,
    expert_ids,
    slot_ids,
    expert_preact,
    conv_weight,
    norm_gain,
    centroids,
    w_in,
    w_out,
):
    sections = lax.axis_size("section")
    section = lax.axis_index("section")
    experts = centroids.shape[1]
    width = centroids.shape[2]
    micros, frames = expert_ids.shape[1:]
    slots, hidden = expert_preact.shape[2:]
    cap = slots // experts
    is_odd = section % 2 == 1

    ids, slot_pos = expert_ids[0], slot_ids[0]
    taps_b = tiles(conv_weight[0])
    taps = taps_b.astype(F32)
    gain_row = norm_gain.astype(F32)
    grads = tiles(out_grad)
    normed, slope, payload = prep(
        lengths[:, 0], ids, slot_pos, tiles(feat_saved[0]), grads, taps,
        tiles(norm_gain[0]).astype(F32), tiles(centroids[0]), cap,
    )
    gelu, gelu_slope = (part.astype(BF16) for part in gelu_parts(expert_preact[0]))
    cent_b = lax.dynamic_slice_in_dim(centroids[0], lax.axis_index("expert"), 1, 0)
    cent_row = cent_b.astype(F32)

    def upward(array):
        return lax.ppermute(array, "section", [(i, i + 1) for i in range(sections - 1)])

    def mine(pair):
        return jnp.where(is_odd, pair[1], pair[0])

    def other(pair):
        return jnp.where(is_odd, pair[0], pair[1])

    target = ids * cap + slot_pos
    up_w_out = upward(w_out[0, 0])
    up_w_in = upward(w_in[0, 0])
    up_gelu = upward(other(gelu))
    up_gelu_slope = upward(other(gelu_slope))
    up_normed = upward(other(normed))
    up_slope = upward(other(slope))
    packed = jnp.concatenate(
        [
            taps_b.reshape(-1, LANES),
            cent_b.reshape(SUB, LANES),
            norm_gain.reshape(SUB, LANES),
            other(target).astype(BF16).reshape(-1, LANES),
        ]
    )
    up_packed = upward(packed)

    sent = exchange(payload).reshape(experts, -1, SUB, LANES)
    lines = sent[:, micros * cap :].reshape(experts, -1, LANES)
    gate = jnp.stack(
        [lines[:, m * cap : (m + 1) * cap].reshape(slots, LANES) for m in range(micros)]
    )
    up_gate = upward(other(gate))
    back = expert(sent, gate, gelu, gelu_slope, w_out[0, 0], w_in[0, 0], cent_row, gain_row)
    back = exchange(back.reshape(experts, -1, LANES)).reshape(-1, SUB, LANES)
    first_rows = ids * (micros * cap) + lax.iota(jnp.int32, micros)[:, None] * cap + slot_pos
    first = frame(lengths[:, 0], first_rows, back, grads, normed, slope, taps)

    size = taps_b.shape[0] * SUB
    up_taps = up_packed[:size].reshape(taps_b.shape).astype(F32)
    up_cent = up_packed[size : size + SUB].reshape(1, width).astype(F32)
    up_gain = up_packed[size + SUB : size + 2 * SUB].reshape(1, width).astype(F32)
    up_target = up_packed[size + 2 * SUB :].reshape(-1).astype(jnp.int32)
    own = (
        mine(gate), mine(gelu), mine(gelu_slope), w_out[0, 0], w_in[0, 0], cent_row, gain_row,
        mine(target), mine(normed), mine(slope), taps,
    )
    came = (
        up_gate, up_gelu, up_gelu_slope, up_w_out, up_w_in, up_cent, up_gain,
        up_target, up_normed, up_slope, up_taps,
    )
    odd_step = tuple(jnp.where(is_odd, b, a) for a, b in zip(own, came))
    even_step = tuple(jnp.where(is_odd, a, b) for a, b in zip(own, came))
    length = mine(lengths)

    kept = first[1]
    arrived = lax.ppermute(first[0], "section", [(sections - 1, sections - 2)])
    own_out, low_out = first[1], first[0]
    for k in range(1, sections):
        (gate_k, gelu_k, gelu_slope_k, w_out_k, w_in_k, cent_k, gain_k,
         target_k, normed_k, slope_k, taps_k) = odd_step if k % 2 else even_step
        take = (section == sections - 1 - k).astype(jnp.int32)
        sent, grad = bucket(take[None], target_k, kept, arrived, slots)
        sent = exchange(sent.reshape(experts, -1, LANES)).reshape(experts, cap, SUB, LANES)
        back = expert(
            sent, gate_k[None], gelu_k[None], gelu_slope_k[None], w_out_k, w_in_k, cent_k, gain_k
        )
        back = exchange(back.reshape(experts, -1, LANES)).reshape(slots, SUB, LANES)
        kept = frame(
            length, target_k[None], back, grad[None], normed_k[None], slope_k[None], taps_k
        )[0]
        if k < sections - 1:
            arrived = lax.ppermute(kept, "section", [(sections - k, sections - 2 - k)])
        own_out = jnp.where(section == sections - 1 - k, kept, own_out)
        low_out = jnp.where(section == sections - k, kept, low_out)
    top = section == sections - 1
    fetched = lax.ppermute(low_out, "section", [(i, i - 1) for i in range(1, sections)])
    rest = jnp.where(top, first[0], fetched)
    pair = jnp.stack([jnp.where(is_odd, rest, own_out), jnp.where(is_odd, own_out, rest)])
    return pair.reshape(1, micros, frames, width)


def solution(mesh):
    in_specs = (
        P("section", None, "expert", None),
        P(None, "expert", None),
        P(None, "expert"),
        P("section", None, "expert"),
        P("section", None, "expert"),
        P("section", None, "expert", None),
        P("section", None, None),
        P("section", None),
        P("section", None, None),
        P("section", "expert", None, None),
        P("section", "expert", None, None),
    )
    out_specs = P("section", None, "expert", None)
    return jax.shard_map(
        on_device, mesh=mesh, in_specs=in_specs, out_specs=out_specs, check_vma=False
    )
```

```python
import functools
import math

import jax
import jax.numpy as jnp
from jax import lax
from jax.experimental import pallas as pl
from jax.experimental.pallas import tpu as pltpu
from jax.sharding import PartitionSpec as P


SUB = 8
LANES = 128
BLOCK = 8
F32 = jnp.float32
BF16 = jnp.bfloat16
PARAMS = pltpu.CompilerParams(vmem_limit_bytes=16 * 2**20)
SMEM = pl.BlockSpec(memory_space=pltpu.SMEM)
VMEM = pl.BlockSpec(memory_space=pltpu.VMEM)


def gelu_parts(preact):
    act_val = preact.astype(F32)
    cdf_val = 0.5 * (1.0 + lax.erf(act_val * (1.0 / math.sqrt(2.0))))
    gelu_val = act_val * cdf_val
    gelu_slope = cdf_val + act_val * jnp.exp(-0.5 * act_val * act_val) * (
        1.0 / math.sqrt(2.0 * math.pi)
    )
    return gelu_val.astype(BF16), gelu_slope.astype(BF16)


def conv_block(src_ref, taps_ref, base, reverse):
    count = taps_ref.shape[0]
    acc = [None] * BLOCK
    for j in range(BLOCK + count - 1):
        at = j + 1 if reverse else j
        row = src_ref[base + at]
        for i in range(BLOCK):
            k = i + count - at if reverse else at - i
            if 0 <= k < count:
                term = taps_ref[k] * row
                acc[i] = term if acc[i] is None else acc[i] + term
    return jnp.stack(acc)


def tile_sum(array):
    return jnp.sum(jnp.sum(array, axis=1, keepdims=True), axis=2, keepdims=True)


def clear_edges(padded, half):
    edge = jnp.zeros((half,) + padded.shape[1:], F32)
    padded[pl.ds(0, half)] = edge
    padded[pl.ds(padded.shape[0] - half, half)] = edge


def block_time(base):
    return base + lax.broadcasted_iota(jnp.int32, (BLOCK, SUB, LANES), 0)


def to_tiles(flat_ref, rows):
    count = rows.shape[0]
    for q in range(SUB):
        flat_ref[pl.ds(q, count, stride=SUB), :] = rows[:, q * LANES : (q + 1) * LANES].astype(F32)


def prep_kernel(
    cap,
    odd_ref,
    len_ref,
    ids_ref,
    slot_ref,
    feat_ref,
    grad_ref,
    taps_ref,
    gain_ref,
    cent_ref,
    *refs,
):
    normed_refs, slope_refs, grads_refs = refs[0:2], refs[2:4], refs[4:6]
    taps_out, pay_ref, padded, flat, cents, gain_flat, info = refs[6:]
    micros, frames = ids_ref.shape
    half = taps_ref.shape[0] // 2
    experts, channels = cent_ref.shape
    per_expert = pay_ref.shape[0] // experts
    info_tiles = per_expert - micros * cap
    pay_ref[...] = jnp.zeros_like(pay_ref)
    info[...] = jnp.zeros_like(info)
    clear_edges(padded, half)
    to_tiles(flat, taps_ref[...])
    taps_out[...] = flat[pl.ds(0, taps_ref.shape[0] * SUB), :].reshape(taps_out.shape)
    to_tiles(cents, cent_ref[...])
    to_tiles(gain_flat, gain_ref[...])
    gain = gain_flat[...][None]
    lane = lax.broadcasted_iota(jnp.int32, (BLOCK, 1, LANES), 2)

    for s in range(micros):
        m = s ^ odd_ref[0]
        length = len_ref[m]
        to_tiles(flat, grad_ref[m])

        def place(block, _, s=s, m=m):
            base = block * BLOCK
            rows = flat[pl.ds(pl.multiple_of(base * SUB, BLOCK * SUB), BLOCK * SUB), :]
            rows = rows.reshape(BLOCK, SUB, LANES).astype(BF16)
            grads_refs[s][pl.ds(base, BLOCK)] = rows
            for i in range(BLOCK):
                at = ids_ref[m, base + i] * per_expert + s * cap + slot_ref[m, base + i]
                pay_ref[at] = rows[i]
            return 0

        lax.fori_loop(0, frames // BLOCK, place, 0)
        to_tiles(flat, feat_ref[m])

        def fill(block, _, length=length):
            base = block * BLOCK
            rows = flat[pl.ds(pl.multiple_of(base * SUB, BLOCK * SUB), BLOCK * SUB), :]
            rows = rows.reshape(BLOCK, SUB, LANES)
            padded[pl.ds(half + base, BLOCK)] = jnp.where(block_time(base) < length, rows, 0.0)
            return 0

        lax.fori_loop(0, frames // BLOCK, fill, 0)

        def step(block, _, s=s, m=m, length=length):
            base = block * BLOCK
            mask = (block_time(base) < length).astype(F32)
            pre = conv_block(padded, taps_out, base, False)
            sig = 1.0 / (1.0 + jnp.exp(-pre))
            rows = flat[pl.ds(pl.multiple_of(base * SUB, BLOCK * SUB), BLOCK * SUB), :]
            residual = rows.reshape(BLOCK, SUB, LANES) + mask * pre * sig
            inv = lax.rsqrt(tile_sum(residual * residual) * (1.0 / channels) + 1e-6)
            scaled = residual * inv
            normed_refs[s][pl.ds(base, BLOCK)] = scaled.astype(BF16)
            slope_refs[s][pl.ds(base, BLOCK)] = (
                mask * sig * (1.0 + pre * (1.0 - sig))
            ).astype(BF16)
            normed = (scaled * gain).astype(BF16).astype(F32)
            lines = jnp.stack(
                [
                    cents[pl.ds(pl.multiple_of(ids_ref[m, base + i] * SUB, SUB), SUB), :]
                    for i in range(BLOCK)
                ]
            )
            gate = 1.0 / (1.0 + jnp.exp(-tile_sum(normed * lines)))
            first = inv * gate
            second = first * (1.0 - gate)
            first_hi = first.astype(BF16).astype(F32)
            second_hi = second.astype(BF16).astype(F32)
            line = jnp.where(lane == 0, first_hi, 0.0)
            line = jnp.where(lane == 1, first - first_hi, line)
            line = jnp.where(lane == 2, second_hi, line)
            line = jnp.where(lane == 3, second - second_hi, line)
            for i in range(BLOCK):
                at = ids_ref[m, base + i] * (info_tiles * SUB) + s * cap + slot_ref[m, base + i]
                info[pl.ds(at, 1), :] = line[i]
            return 0

        lax.fori_loop(0, frames // BLOCK, step, 0)

    def put_info(expert, _):
        for t in range(info_tiles):
            rows = info[pl.ds(pl.multiple_of((expert * info_tiles + t) * SUB, SUB), SUB), :]
            pay_ref[expert * per_expert + micros * cap + t] = rows.astype(BF16)
        return 0

    lax.fori_loop(0, experts, put_info, 0, unroll=4)


def prep(odd, lengths, ids, slots, feats, grads, taps, gain, cents, cap):
    micros, frames = ids.shape
    experts = cents.shape[0]
    info_tiles = -(-micros * cap // SUB)
    per_expert = micros * cap + info_tiles
    count = taps.shape[0]
    one = jax.ShapeDtypeStruct((frames, SUB, LANES), BF16)
    outs = pl.pallas_call(
        functools.partial(prep_kernel, cap),
        out_shape=(one,) * 6
        + (
            jax.ShapeDtypeStruct((count, SUB, LANES), F32),
            jax.ShapeDtypeStruct((experts * per_expert, SUB, LANES), BF16),
        ),
        in_specs=[SMEM] * 4 + [VMEM] * 5,
        out_specs=[VMEM] * 8,
        scratch_shapes=[
            pltpu.VMEM((frames + count, SUB, LANES), F32),
            pltpu.VMEM((max(frames, count) * SUB, LANES), F32),
            pltpu.VMEM((experts * SUB, LANES), F32),
            pltpu.VMEM((SUB, LANES), F32),
            pltpu.VMEM((experts * info_tiles * SUB, LANES), F32),
        ],
        name="prep",
    )(odd, lengths, ids, slots, feats, grads, taps, gain, cents)
    payload = outs[7].reshape(experts, per_expert * SUB, LANES)
    return outs[0:2], outs[2:4], outs[4:6], outs[6], payload


def expert_rows(rows, gate, gelu_ref, slope_ref, w_out_ref, w_in_ref, cent_ref, gain_ref, wide, left):
    slots = left.shape[0]
    wide[...] = rows.reshape(wide.shape).astype(F32)
    for q in range(SUB):
        left[:, q * LANES : (q + 1) * LANES] = wide[pl.ds(q, slots, stride=SUB), :].astype(BF16)
    dims = (((1,), (1,)), ((), ()))
    first = gate[:, 0:1] + gate[:, 1:2]
    second = gate[:, 2:3] + gate[:, 3:4]
    hidden = lax.dot_general(left[...], w_out_ref[...], dims, preferred_element_type=F32)
    pre_grad = (hidden * slope_ref[...].astype(F32) * first).astype(BF16)
    total = lax.dot_general(pre_grad, w_in_ref[...], dims, preferred_element_type=F32)
    weight = second * jnp.sum(hidden * gelu_ref[...].astype(F32), axis=1, keepdims=True)
    for q in range(SUB):
        cols = slice(q * LANES, (q + 1) * LANES)
        wide[pl.ds(q, slots, stride=SUB), :] = (
            total[:, cols] + weight * cent_ref[:, cols]
        ) * gain_ref[:, cols]
    return wide[...].astype(BF16)


def expert_kernel(rows_ref, gate_ref, *refs):
    out_ref, wide, left = refs[6:]
    gate = gate_ref[...].astype(F32)
    out_ref[...] = expert_rows(rows_ref[...], gate, *refs[:6], wide, left).reshape(out_ref.shape)


def expert(rows, gate, *operands):
    slots = gate.shape[0]
    width = operands[3].shape[0]
    return pl.pallas_call(
        expert_kernel,
        out_shape=jax.ShapeDtypeStruct(rows.shape, BF16),
        in_specs=[VMEM] * 8,
        out_specs=VMEM,
        scratch_shapes=[pltpu.VMEM((slots * SUB, LANES), F32), pltpu.VMEM((slots, width), BF16)],
        compiler_params=PARAMS,
        name="expert",
    )(rows, gate, *operands)


def first_expert_kernel(rows_ref, *refs):
    gelu_refs, slope_refs, shared = refs[0:2], refs[2:4], refs[4:8]
    out_ref, gate_refs, wide, left, info, gate = refs[8], refs[9:11], *refs[11:]
    devices, tiles = rows_ref.shape[:2]
    cap = left.shape[0] // devices
    micros = len(gelu_refs)
    per_device = (tiles - micros * cap) * SUB
    info[...] = rows_ref[:, micros * cap :].reshape(info.shape).astype(F32)
    for s in range(micros):
        for j in range(cap):
            gate[pl.ds(j, devices, stride=cap), :] = info[
                pl.ds(s * cap + j, devices, stride=per_device), :
            ]
        gate_refs[s][...] = gate[...].astype(BF16)
        back = expert_rows(
            rows_ref[:, s * cap : (s + 1) * cap],
            gate[...], gelu_refs[s], slope_refs[s], *shared, wide, left,
        )
        out_ref[:, s * cap : (s + 1) * cap] = back.reshape(devices, cap, SUB, LANES)


def first_expert(rows, gelus, slopes, *shared):
    slots = gelus[0].shape[0]
    devices, tiles = rows.shape[:2]
    width = shared[1].shape[0]
    micros = len(gelus)
    shown = micros * slots // devices
    line = jax.ShapeDtypeStruct((slots, LANES), BF16)
    return pl.pallas_call(
        first_expert_kernel,
        out_shape=(jax.ShapeDtypeStruct((devices, shown, SUB, LANES), BF16), line, line),
        in_specs=[VMEM] * 9,
        out_specs=[VMEM] * 3,
        scratch_shapes=[
            pltpu.VMEM((slots * SUB, LANES), F32),
            pltpu.VMEM((slots, width), BF16),
            pltpu.VMEM((devices * (tiles - shown) * SUB, LANES), F32),
            pltpu.VMEM((slots, LANES), F32),
        ],
        compiler_params=PARAMS,
        name="first_expert",
    )(rows, *gelus, *slopes, *shared)


def frame_kernel(
    take_ref, len_ref, row_ref, back_ref, kept_ref, came_ref, normed_ref, slope_ref, taps_ref,
    out_ref, held, padded,
):
    frames = kept_ref.shape[0]
    half = taps_ref.shape[0] // 2
    channels = kept_ref.shape[1] * kept_ref.shape[2]
    length = len_ref[0]
    take = take_ref[0] != 0
    clear_edges(padded, half)

    def norm(block, _):
        base = block * BLOCK
        rows = pl.ds(base, BLOCK)
        back = jnp.stack([back_ref[row_ref[base + i]].astype(F32) for i in range(BLOCK)])
        normed = normed_ref[rows].astype(F32)
        mean = tile_sum(normed * back) * (1.0 / channels)
        grad = jnp.where(take, came_ref[rows].astype(F32), kept_ref[rows].astype(F32))
        resid = grad + back - normed * mean
        held[rows] = resid
        padded[pl.ds(half + base, BLOCK)] = resid * slope_ref[rows].astype(F32)
        return 0

    lax.fori_loop(0, frames // BLOCK, norm, 0, unroll=4)

    def conv(block, _):
        base = block * BLOCK
        summed = conv_block(padded, taps_ref, base, True)
        resid = held[pl.ds(base, BLOCK)]
        out = jnp.where(block_time(base) < length, resid + summed, resid)
        out_ref[pl.ds(base, BLOCK)] = out.astype(BF16)
        return 0

    lax.fori_loop(0, frames // BLOCK, conv, 0)


def frame(take, length, rows, back, kept, came, normed, slope, taps):
    frames = kept.shape[0]
    return pl.pallas_call(
        frame_kernel,
        out_shape=jax.ShapeDtypeStruct(kept.shape, BF16),
        in_specs=[SMEM] * 3 + [VMEM] * 6,
        out_specs=VMEM,
        scratch_shapes=[
            pltpu.VMEM((frames, SUB, LANES), F32),
            pltpu.VMEM((frames + taps.shape[0], SUB, LANES), F32),
        ],
        compiler_params=PARAMS,
        name="frame",
    )(take, length, rows, back, kept, came, normed, slope, taps)


def bucket_kernel(take_ref, row_ref, kept_ref, came_ref, bucket_ref):
    frames = kept_ref.shape[0]
    bucket_ref[...] = jnp.zeros_like(bucket_ref)

    def move(source):
        def step(block, _):
            base = block * BLOCK
            for i in range(BLOCK):
                bucket_ref[row_ref[base + i]] = source[base + i]
            return 0

        lax.fori_loop(0, frames // BLOCK, step, 0)

    @pl.when(take_ref[0] != 0)
    def _():
        move(came_ref)

    @pl.when(take_ref[0] == 0)
    def _():
        move(kept_ref)


def bucket(take, rows, kept, came, slots):
    return pl.pallas_call(
        bucket_kernel,
        out_shape=jax.ShapeDtypeStruct((slots, SUB, LANES), BF16),
        in_specs=[SMEM, SMEM, VMEM, VMEM],
        out_specs=VMEM,
        compiler_params=PARAMS,
        name="bucket",
    )(take, rows, kept, came)


def exchange(array):
    return lax.all_to_all(array, "expert", split_axis=0, concat_axis=0, tiled=True)


def on_device(
    feat_saved,
    out_grad,
    lengths,
    expert_ids,
    slot_ids,
    expert_preact,
    conv_weight,
    norm_gain,
    centroids,
    w_in,
    w_out,
):
    sections = lax.axis_size("section")
    section = lax.axis_index("section")
    experts, width = centroids.shape[1:]
    micros, frames = expert_ids.shape[1:]
    slots = expert_preact.shape[2]
    cap = slots // experts
    odd = section % 2
    is_odd = odd == 1

    def upward(array):
        return lax.ppermute(array, "section", [(i, i + 1) for i in range(sections - 1)])

    def pick(array, which):
        return lax.dynamic_index_in_dim(array, which, 0, keepdims=False)

    own_w_out, own_w_in = w_out[0, 0], w_in[0, 0]
    up_w_out = upward(own_w_out)
    up_w_in = upward(own_w_in)
    gain_row = norm_gain.astype(F32)
    cent_b = lax.dynamic_slice_in_dim(centroids[0], lax.axis_index("expert"), 1, 0)
    cent_row = cent_b.astype(F32)
    normed, slope, grads, taps, payload = prep(
        odd[None], lengths[:, 0], expert_ids[0], slot_ids[0], feat_saved[0], out_grad,
        conv_weight[0], norm_gain, centroids[0], cap,
    )
    gelu, gelu_slope = zip(
        *(gelu_parts(pick(expert_preact[0], which)) for which in (odd, 1 - odd))
    )

    ids = [pick(expert_ids[0], which) for which in (odd, 1 - odd)]
    slot_pos = [pick(slot_ids[0], which) for which in (odd, 1 - odd)]
    target = [i * cap + s for i, s in zip(ids, slot_pos)]
    packed = jnp.concatenate(
        [
            taps.astype(BF16).reshape(-1, LANES),
            cent_b.reshape(SUB, LANES),
            norm_gain.reshape(SUB, LANES),
            target[1].astype(BF16).reshape(-1, LANES),
        ]
    )
    up_gelu = upward(gelu[1])
    up_gelu_slope = upward(gelu_slope[1])
    up_packed = upward(packed)
    up_normed = upward(normed[1])
    up_slope = upward(slope[1])

    sent = exchange(payload).reshape(experts, -1, SUB, LANES)
    back, gate, other_gate = first_expert(
        sent, gelu, gelu_slope, own_w_out, own_w_in, cent_row, gain_row
    )
    up_gate = upward(other_gate)
    back = exchange(back.reshape(experts, -1, LANES)).reshape(-1, SUB, LANES)
    none = jnp.zeros((1,), jnp.int32)
    own_length = pick(lengths, odd)
    first = [None, None]
    for s in (1, 0):
        rows = ids[s] * (micros * cap) + s * cap + slot_pos[s]
        first[s] = frame(
            none, pick(lengths, 1 - odd) if s else own_length, rows, back,
            grads[s], grads[s], normed[s], slope[s], taps,
        )
        if s:
            arrived = lax.ppermute(first[s], "section", [(sections - 1, sections - 2)])
    kept = first[0]

    size = taps.shape[0] * SUB
    came = (
        up_gate,
        up_gelu,
        up_gelu_slope,
        up_w_out,
        up_w_in,
        up_packed[size : size + SUB].reshape(1, width).astype(F32),
        up_packed[size + SUB : size + 2 * SUB].reshape(1, width).astype(F32),
        up_packed[size + 2 * SUB :].reshape(-1).astype(jnp.int32),
        up_normed,
        up_slope,
        up_packed[:size].reshape(taps.shape).astype(F32),
    )
    own = (
        gate, gelu[0], gelu_slope[0], own_w_out, own_w_in, cent_row, gain_row,
        target[0], normed[0], slope[0], taps,
    )
    own = lax.optimization_barrier(own)
    steps = {1: tuple(jnp.where(is_odd, b, a) for a, b in zip(own, came))}

    own_out = low_out = kept
    for k in range(1, sections):
        if k == 2:
            own, came, kept = lax.optimization_barrier((own, came, kept))
            steps[0] = tuple(jnp.where(is_odd, a, b) for a, b in zip(own, came))
        operands = steps[k % 2]
        rows = operands[7]
        take = (section == sections - 1 - k).astype(jnp.int32)[None]
        sent = bucket(take, rows, kept, arrived, slots)
        sent = exchange(sent.reshape(experts, -1, LANES)).reshape(experts, cap, SUB, LANES)
        back = expert(sent, *operands[:7])
        back = exchange(back.reshape(experts, -1, LANES)).reshape(slots, SUB, LANES)
        kept = frame(take, own_length, rows, back, kept, arrived, *operands[8:])
        if k < sections - 1:
            arrived = lax.ppermute(kept, "section", [(sections - k, sections - 2 - k)])
        own_out = jnp.where(section == sections - 1 - k, kept, own_out)
        low_out = jnp.where(section == sections - k, kept, low_out)
    fetched = lax.ppermute(low_out, "section", [(i, i - 1) for i in range(1, sections)])
    rest = jnp.where(section == sections - 1, first[1], fetched)
    pair = jnp.stack([jnp.where(is_odd, rest, own_out), jnp.where(is_odd, own_out, rest)])
    return pair.reshape(1, micros, frames, width)


def solution(mesh):
    in_specs = (
        P("section", None, "expert", None),
        P(None, "expert", None),
        P(None, "expert"),
        P("section", None, "expert"),
        P("section", None, "expert"),
        P("section", None, "expert", None),
        P("section", None, None),
        P("section", None),
        P("section", None, None),
        P("section", "expert", None, None),
        P("section", "expert", None, None),
    )
    out_specs = P("section", None, "expert", None)

    return jax.shard_map(
        on_device, mesh=mesh, in_specs=in_specs, out_specs=out_specs, check_vma=False
    )
```

```python
import functools
import math

import jax
import jax.numpy as jnp
from jax import lax
from jax.experimental import pallas as pl
from jax.experimental.pallas import tpu as pltpu
from jax.sharding import PartitionSpec as P


SUB = 8
LANES = 128
BLOCK = 8
UNROLL = 4
F32 = jnp.float32
BF16 = jnp.bfloat16
PARAMS = pltpu.CompilerParams(vmem_limit_bytes=16 * 2**20)
SMEM = pl.BlockSpec(memory_space=pltpu.SMEM)
VMEM = pl.BlockSpec(memory_space=pltpu.VMEM)
HBM = pl.BlockSpec(memory_space=pltpu.HBM)


def gelu_parts(preact):
    act_val = preact.astype(F32)
    cdf_val = 0.5 * (1.0 + lax.erf(act_val * (1.0 / math.sqrt(2.0))))
    gelu_val = act_val * cdf_val
    gelu_slope = cdf_val + act_val * jnp.exp(-0.5 * act_val * act_val) * (
        1.0 / math.sqrt(2.0 * math.pi)
    )
    return gelu_val.astype(BF16), gelu_slope.astype(BF16)


def conv_block(src_ref, taps_ref, base, reverse):
    count = taps_ref.shape[0]
    acc = [None] * BLOCK
    for j in range(BLOCK + count - 1):
        at = j + 1 if reverse else j
        row = src_ref[base + at]
        for i in range(BLOCK):
            k = i + count - at if reverse else at - i
            if 0 <= k < count:
                term = taps_ref[k] * row
                acc[i] = term if acc[i] is None else acc[i] + term
    return jnp.stack(acc)


def tile_sum(array):
    return jnp.sum(jnp.sum(array, axis=1, keepdims=True), axis=2, keepdims=True)


def clear_edges(padded, half):
    edge = jnp.zeros((half,) + padded.shape[1:], F32)
    padded[pl.ds(0, half)] = edge
    padded[pl.ds(padded.shape[0] - half, half)] = edge


def block_time(base):
    return base + lax.broadcasted_iota(jnp.int32, (BLOCK, SUB, LANES), 0)


def to_tiles(flat_ref, rows):
    count = rows.shape[0]
    for q in range(SUB):
        flat_ref[pl.ds(q, count, stride=SUB), :] = rows[:, q * LANES : (q + 1) * LANES].astype(F32)


def prep_kernel(
    cap,
    place_ref,
    len_ref,
    ids_ref,
    slot_ref,
    feat_ref,
    grad_ref,
    taps_ref,
    gain_ref,
    cent_ref,
    *refs,
):
    normed_refs, slope_refs, grads_refs = refs[0:2], refs[2:4], refs[4:6]
    packed_ref, pay_ref, taps, padded, flat, cents, gain_flat, info = refs[6:]
    micros, frames = ids_ref.shape
    half = taps_ref.shape[0] // 2
    experts, channels = cent_ref.shape
    per_expert = pay_ref.shape[0] // experts
    info_tiles = per_expert - micros * cap
    pay_ref[...] = jnp.zeros_like(pay_ref)
    info[...] = jnp.zeros_like(info)
    clear_edges(padded, half)
    to_tiles(flat, taps_ref[...])
    size = taps_ref.shape[0] * SUB
    taps[...] = flat[pl.ds(0, size), :].reshape(taps.shape)
    to_tiles(cents, cent_ref[...])
    to_tiles(gain_flat, gain_ref[...])
    packed_ref[pl.ds(0, size), :] = flat[pl.ds(0, size), :].astype(BF16)
    mine = pl.ds(pl.multiple_of(place_ref[1] * SUB, SUB), SUB)
    packed_ref[pl.ds(size, 2 * SUB), :] = jnp.concatenate(
        [cents[mine, :], gain_flat[...]]
    ).astype(BF16)
    gain = gain_flat[...][None]
    lane = lax.broadcasted_iota(jnp.int32, (BLOCK, 1, LANES), 2)

    for s in range(micros):
        m = s ^ place_ref[0]
        length = len_ref[m]
        to_tiles(flat, grad_ref[m])

        def place(block, _, s=s, m=m):
            base = block * BLOCK
            rows = flat[pl.ds(pl.multiple_of(base * SUB, BLOCK * SUB), BLOCK * SUB), :]
            rows = rows.reshape(BLOCK, SUB, LANES).astype(BF16)
            grads_refs[s][pl.ds(base, BLOCK)] = rows
            for i in range(BLOCK):
                at = ids_ref[m, base + i] * per_expert + s * cap + slot_ref[m, base + i]
                pay_ref[at] = rows[i]
            return 0

        lax.fori_loop(0, frames // BLOCK, place, 0, unroll=2)
        to_tiles(flat, feat_ref[m])

        def fill(block, _, length=length):
            base = block * BLOCK
            rows = flat[pl.ds(pl.multiple_of(base * SUB, BLOCK * SUB), BLOCK * SUB), :]
            rows = rows.reshape(BLOCK, SUB, LANES)
            padded[pl.ds(half + base, BLOCK)] = jnp.where(block_time(base) < length, rows, 0.0)
            return 0

        lax.fori_loop(0, frames // BLOCK, fill, 0, unroll=2)

        def step(block, _, s=s, m=m, length=length):
            base = block * BLOCK
            mask = (block_time(base) < length).astype(F32)
            pre = conv_block(padded, taps, base, False)
            sig = 1.0 / (1.0 + jnp.exp(-pre))
            rows = flat[pl.ds(pl.multiple_of(base * SUB, BLOCK * SUB), BLOCK * SUB), :]
            residual = rows.reshape(BLOCK, SUB, LANES) + mask * pre * sig
            inv = lax.rsqrt(tile_sum(residual * residual) * (1.0 / channels) + 1e-6)
            scaled = residual * inv
            normed_refs[s][pl.ds(base, BLOCK)] = scaled.astype(BF16)
            slope_refs[s][pl.ds(base, BLOCK)] = (
                mask * sig * (1.0 + pre * (1.0 - sig))
            ).astype(BF16)
            normed = (scaled * gain).astype(BF16).astype(F32)
            lines = jnp.stack(
                [
                    cents[pl.ds(pl.multiple_of(ids_ref[m, base + i] * SUB, SUB), SUB), :]
                    for i in range(BLOCK)
                ]
            )
            gate = 1.0 / (1.0 + jnp.exp(-tile_sum(normed * lines)))
            first = inv * gate
            second = first * (1.0 - gate)
            first_hi = first.astype(BF16).astype(F32)
            second_hi = second.astype(BF16).astype(F32)
            line = jnp.where(lane == 0, first_hi, 0.0)
            line = jnp.where(lane == 1, first - first_hi, line)
            line = jnp.where(lane == 2, second_hi, line)
            line = jnp.where(lane == 3, second - second_hi, line)
            for i in range(BLOCK):
                at = ids_ref[m, base + i] * (info_tiles * SUB) + s * cap + slot_ref[m, base + i]
                info[pl.ds(at, 1), :] = line[i]
            return 0

        lax.fori_loop(0, frames // BLOCK, step, 0, unroll=UNROLL)

    def put_info(expert, _):
        for t in range(info_tiles):
            rows = info[pl.ds(pl.multiple_of((expert * info_tiles + t) * SUB, SUB), SUB), :]
            pay_ref[expert * per_expert + micros * cap + t] = rows.astype(BF16)
        return 0

    lax.fori_loop(0, experts, put_info, 0, unroll=4)


def prep(place, lengths, ids, slots, feats, grads, taps, gain, cents, cap):
    micros, frames = ids.shape
    experts = cents.shape[0]
    info_tiles = -(-micros * cap // SUB)
    per_expert = micros * cap + info_tiles
    count = taps.shape[0]
    one = jax.ShapeDtypeStruct((frames, SUB, LANES), BF16)
    outs = pl.pallas_call(
        functools.partial(prep_kernel, cap),
        out_shape=(one,) * 6
        + (
            jax.ShapeDtypeStruct(((count + 2) * SUB, LANES), BF16),
            jax.ShapeDtypeStruct((experts * per_expert, SUB, LANES), BF16),
        ),
        in_specs=[SMEM] * 4 + [VMEM] * 5,
        out_specs=[VMEM] * 8,
        scratch_shapes=[
            pltpu.VMEM((count, SUB, LANES), F32),
            pltpu.VMEM((frames + count, SUB, LANES), F32),
            pltpu.VMEM((max(frames, count) * SUB, LANES), F32),
            pltpu.VMEM((experts * SUB, LANES), F32),
            pltpu.VMEM((SUB, LANES), F32),
            pltpu.VMEM((experts * info_tiles * SUB, LANES), F32),
        ],
        name="prep",
    )(place, lengths, ids, slots, feats, grads, taps, gain, cents)
    payload = outs[7].reshape(experts, per_expert * SUB, LANES)
    return outs[0:2], outs[2:4], outs[4:6], outs[6], payload


def fetch(sources, targets, sems):
    copies = [
        pltpu.make_async_copy(source, target, sems.at[i])
        for i, (source, target) in enumerate(zip(sources, targets))
    ]
    for copy in copies:
        copy.start()
    return [copy.wait for copy in copies]


def expert_rows(rows, gate, gelu_ref, slope_ref, w_out_ref, w_in_ref, packed_ref, wide, left):
    slots = left.shape[0]
    wide[...] = rows.reshape(wide.shape).astype(F32)
    for q in range(SUB):
        left[:, q * LANES : (q + 1) * LANES] = wide[pl.ds(q, slots, stride=SUB), :].astype(BF16)
    dims = (((1,), (1,)), ((), ()))
    first = gate[:, 0:1] + gate[:, 1:2]
    second = gate[:, 2:3] + gate[:, 3:4]
    hidden = lax.dot_general(left[...], w_out_ref[...], dims, preferred_element_type=F32)
    pre_grad = (hidden * slope_ref[...].astype(F32) * first).astype(BF16)
    total = lax.dot_general(pre_grad, w_in_ref[...], dims, preferred_element_type=F32)
    weight = second * jnp.sum(hidden * gelu_ref[...].astype(F32), axis=1, keepdims=True)
    size = packed_ref.shape[0] - 2 * SUB
    cent_gain = packed_ref[pl.ds(size, 2 * SUB), :].astype(F32)
    for q in range(SUB):
        wide[pl.ds(q, slots, stride=SUB), :] = (
            total[:, q * LANES : (q + 1) * LANES] + weight * cent_gain[q : q + 1]
        ) * cent_gain[SUB + q : SUB + q + 1]
    return wide[...].astype(BF16)


def expert_kernel(rows_ref, gate_ref, *refs):
    out_ref, wide, left = refs[5:]
    gate = gate_ref[...].astype(F32)
    out_ref[...] = expert_rows(rows_ref[...], gate, *refs[:5], wide, left).reshape(out_ref.shape)


def expert(rows, gate, *operands):
    slots = gate.shape[0]
    width = operands[3].shape[0]
    return pl.pallas_call(
        expert_kernel,
        out_shape=jax.ShapeDtypeStruct(rows.shape, BF16),
        in_specs=[VMEM] * 7,
        out_specs=VMEM,
        scratch_shapes=[pltpu.VMEM((slots * SUB, LANES), F32), pltpu.VMEM((slots, width), BF16)],
        compiler_params=PARAMS,
        name="expert",
    )(rows, gate, *operands)


def first_expert_kernel(rows_ref, *refs):
    gelu_refs, slope_refs, shared = refs[0:2], refs[2:4], refs[4:7]
    out_ref, gate_refs, wide, left, info, gate = refs[7], refs[8:10], *refs[10:]
    devices, tiles = rows_ref.shape[:2]
    cap = left.shape[0] // devices
    micros = len(gelu_refs)
    per_device = (tiles - micros * cap) * SUB
    info[...] = rows_ref[:, micros * cap :].reshape(info.shape).astype(F32)
    for s in range(micros):
        for j in range(cap):
            gate[pl.ds(j, devices, stride=cap), :] = info[
                pl.ds(s * cap + j, devices, stride=per_device), :
            ]
        gate_refs[s][...] = gate[...].astype(BF16)
        back = expert_rows(
            rows_ref[:, s * cap : (s + 1) * cap],
            gate[...], gelu_refs[s], slope_refs[s], *shared, wide, left,
        )
        out_ref[:, s * cap : (s + 1) * cap] = back.reshape(devices, cap, SUB, LANES)


def first_expert(rows, gelus, slopes, *shared):
    slots = gelus[0].shape[0]
    devices, tiles = rows.shape[:2]
    width = shared[1].shape[0]
    micros = len(gelus)
    shown = micros * slots // devices
    line = jax.ShapeDtypeStruct((slots, LANES), BF16)
    return pl.pallas_call(
        first_expert_kernel,
        out_shape=(jax.ShapeDtypeStruct((devices, shown, SUB, LANES), BF16), line, line),
        in_specs=[VMEM] * 8,
        out_specs=[VMEM] * 3,
        scratch_shapes=[
            pltpu.VMEM((slots * SUB, LANES), F32),
            pltpu.VMEM((slots, width), BF16),
            pltpu.VMEM((devices * (tiles - shown) * SUB, LANES), F32),
            pltpu.VMEM((slots, LANES), F32),
        ],
        compiler_params=PARAMS,
        name="first_expert",
    )(rows, *gelus, *slopes, *shared)


def frame_kernel(
    taker, which, back_ref, kept_ref, came_ref, normed_ref, slope_ref, packed_ref, lines_hbm,
    out_ref, held, padded, taps_ref, line_ref, sems,
):
    (wait,) = fetch((lines_hbm.at[which],), (line_ref,), sems)
    taps_ref[...] = packed_ref[pl.ds(0, taps_ref.shape[0] * SUB), :].astype(F32).reshape(
        taps_ref.shape
    )
    frames = kept_ref.shape[0]
    half = taps_ref.shape[0] // 2
    channels = kept_ref.shape[1] * kept_ref.shape[2]
    clear_edges(padded, half)
    wait()
    length = line_ref[1, 0]
    take = line_ref[1, 1] == taker

    def norm(block, _):
        base = block * BLOCK
        rows = pl.ds(base, BLOCK)
        back = jnp.stack([back_ref[line_ref[0, base + i]].astype(F32) for i in range(BLOCK)])
        normed = normed_ref[rows].astype(F32)
        mean = tile_sum(normed * back) * (1.0 / channels)
        grad = jnp.where(take, came_ref[rows].astype(F32), kept_ref[rows].astype(F32))
        resid = grad + back - normed * mean
        held[rows] = resid
        padded[pl.ds(half + base, BLOCK)] = resid * slope_ref[rows].astype(F32)
        return 0

    lax.fori_loop(0, frames // BLOCK, norm, 0, unroll=4)

    def conv(block, _):
        base = block * BLOCK
        summed = conv_block(padded, taps_ref, base, True)
        resid = held[pl.ds(base, BLOCK)]
        out = jnp.where(block_time(base) < length, resid + summed, resid)
        out_ref[pl.ds(base, BLOCK)] = out.astype(BF16)
        return 0

    lax.fori_loop(0, frames // BLOCK, conv, 0)


def frame(taker, which, lines, back, kept, came, normed, slope, packed):
    frames = kept.shape[0]
    count = packed.shape[0] // SUB - 2
    return pl.pallas_call(
        functools.partial(frame_kernel, taker, which),
        out_shape=jax.ShapeDtypeStruct(kept.shape, BF16),
        in_specs=[VMEM] * 6 + [HBM],
        out_specs=VMEM,
        scratch_shapes=[
            pltpu.VMEM((frames, SUB, LANES), F32),
            pltpu.VMEM((frames + count, SUB, LANES), F32),
            pltpu.VMEM((count, SUB, LANES), F32),
            pltpu.SMEM(lines.shape[1:], lines.dtype),
            pltpu.SemaphoreType.DMA((1,)),
        ],
        compiler_params=PARAMS,
        name="frame",
    )(back, kept, came, normed, slope, packed, lines)


def bucket_kernel(taker, which, kept_ref, came_ref, lines_hbm, bucket_ref, line_ref, sems):
    (wait,) = fetch((lines_hbm.at[which],), (line_ref,), sems)
    frames = kept_ref.shape[0]
    bucket_ref[...] = jnp.zeros_like(bucket_ref)
    wait()
    take = line_ref[1, 1] == taker

    def move(source):
        def step(block, _):
            base = block * BLOCK
            for i in range(BLOCK):
                bucket_ref[line_ref[0, base + i]] = source[base + i]
            return 0

        lax.fori_loop(0, frames // BLOCK, step, 0)

    @pl.when(take)
    def _():
        move(came_ref)

    @pl.when(jnp.logical_not(take))
    def _():
        move(kept_ref)


def bucket(taker, which, lines, kept, came, slots):
    return pl.pallas_call(
        functools.partial(bucket_kernel, taker, which),
        out_shape=jax.ShapeDtypeStruct((slots, SUB, LANES), BF16),
        in_specs=[VMEM, VMEM, HBM],
        out_specs=VMEM,
        scratch_shapes=[pltpu.SMEM(lines.shape[1:], lines.dtype), pltpu.SemaphoreType.DMA((1,))],
        compiler_params=PARAMS,
        name="bucket",
    )(kept, came, lines)


def choose_kernel(odd_ref, *refs):
    count = (len(refs) - 1) // 4
    own, came, odd_out, even_out = (refs[i * count : (i + 1) * count] for i in range(4))
    sems = refs[-1]

    def run(odd, even):
        waits = fetch(odd, odd_out, sems.at[0]) + fetch(even, even_out, sems.at[1])
        for wait in waits:
            wait()

    @pl.when(odd_ref[0] == 1)
    def _():
        run(came, own)

    @pl.when(odd_ref[0] == 0)
    def _():
        run(own, came)


def choose(odd, own, came):
    count = len(own)
    shapes = tuple(jax.ShapeDtypeStruct(array.shape, array.dtype) for array in own)
    outs = pl.pallas_call(
        choose_kernel,
        out_shape=shapes * 2,
        in_specs=[SMEM] + [HBM] * (2 * count),
        out_specs=[VMEM] * (2 * count),
        scratch_shapes=[pltpu.SemaphoreType.DMA((2, count))],
        compiler_params=pltpu.CompilerParams(vmem_limit_bytes=49 * 2**20),
        name="choose",
    )(odd, *own, *came)
    return outs[count:], outs[:count]


def finish_kernel(place_ref, own_ref, kept_ref, rest_ref, last_ref, out_ref, flat):
    count = own_ref.shape[0]
    for s, (early, late) in enumerate(((own_ref, kept_ref), (rest_ref, last_ref))):

        @pl.when(place_ref[1] == 0)
        def _(late=late):
            flat[...] = late[...].astype(F32).reshape(flat.shape)

        @pl.when(place_ref[1] != 0)
        def _(early=early):
            flat[...] = early[...].astype(F32).reshape(flat.shape)

        m = s ^ place_ref[0]
        for q in range(SUB):
            out_ref[m, :, q * LANES : (q + 1) * LANES] = flat[
                pl.ds(q, count, stride=SUB), :
            ].astype(BF16)


def finish(place, own, kept, rest, last):
    frames = own.shape[0]
    return pl.pallas_call(
        finish_kernel,
        out_shape=jax.ShapeDtypeStruct((2, frames, SUB * LANES), BF16),
        in_specs=[SMEM] + [VMEM] * 4,
        out_specs=VMEM,
        scratch_shapes=[pltpu.VMEM((frames * SUB, LANES), F32)],
        compiler_params=PARAMS,
        name="finish",
    )(place, own, kept, rest, last)


def exchange(array):
    return lax.all_to_all(array, "expert", split_axis=0, concat_axis=0, tiled=True)


def on_device(
    feat_saved,
    out_grad,
    lengths,
    expert_ids,
    slot_ids,
    expert_preact,
    conv_weight,
    norm_gain,
    centroids,
    w_in,
    w_out,
):
    sections = lax.axis_size("section")
    section = lax.axis_index("section")
    experts, _ = centroids.shape[1:]
    micros, frames = expert_ids.shape[1:]
    slots = expert_preact.shape[2]
    cap = slots // experts
    odd = section % 2
    is_odd = odd == 1

    def upward(array):
        return lax.ppermute(array, "section", [(i, i + 1) for i in range(sections - 1)])

    def pick(array, which):
        return lax.dynamic_index_in_dim(array, which, 0, keepdims=False)

    own_w_out, own_w_in = w_out[0, 0], w_in[0, 0]
    up_w_out = upward(own_w_out)
    up_w_in = upward(own_w_in)
    normed, slope, grads, packed, payload = prep(
        jnp.stack([odd, lax.axis_index("expert")]), lengths[:, 0], expert_ids[0], slot_ids[0],
        feat_saved[0], out_grad, conv_weight[0], norm_gain, centroids[0], cap,
    )
    gelu, gelu_slope = zip(
        *(gelu_parts(pick(expert_preact[0], which)) for which in (odd, 1 - odd))
    )

    ids = [pick(expert_ids[0], which) for which in (odd, 1 - odd)]
    slot_pos = [pick(slot_ids[0], which) for which in (odd, 1 - odd)]
    target = [i * cap + s for i, s in zip(ids, slot_pos)]
    up_target = upward(target[1])
    up_gelu = upward(gelu[1])
    up_gelu_slope = upward(gelu_slope[1])
    up_packed = upward(packed)
    up_normed = upward(normed[1])
    up_slope = upward(slope[1])

    def line_of(rows, which):
        tail = jnp.pad(jnp.stack([pick(lengths, which)[0], section]), (0, frames - 2))
        return jnp.stack([rows, tail])

    sent = exchange(payload).reshape(experts, -1, SUB, LANES)
    back, gate, other_gate = first_expert(sent, gelu, gelu_slope, own_w_out, own_w_in, packed)
    up_gate = upward(other_gate)
    back = exchange(back.reshape(experts, -1, LANES)).reshape(-1, SUB, LANES)
    lines = jnp.stack(
        [
            line_of(ids[s] * (micros * cap) + s * cap + slot_pos[s], 1 - odd if s else odd)
            for s in (0, 1)
        ]
    )
    first = [None, None]
    for s in (1, 0):
        first[s] = frame(-1, s, lines, back, grads[s], grads[s], normed[s], slope[s], packed)
        if s:
            arrived = lax.ppermute(first[s], "section", [(sections - 1, sections - 2)])
    kept = first[0]

    mine, came = line_of(target[0], odd), line_of(up_target, odd)
    lines = jnp.stack([jnp.where(is_odd, mine, came), jnp.where(is_odd, came, mine)])
    steps = choose(
        odd[None],
        (gate, gelu[0], gelu_slope[0], own_w_out, own_w_in, packed, normed[0], slope[0]),
        (up_gate, up_gelu, up_gelu_slope, up_w_out, up_w_in, up_packed, up_normed, up_slope),
    )

    own_out = low_out = kept
    for k in range(1, sections):
        (gate_k, gelu_k, gelu_slope_k, w_out_k, w_in_k, packed_k, normed_k, slope_k) = steps[k % 2]
        taker = sections - 1 - k
        sent = bucket(taker, k % 2, lines, kept, arrived, slots)
        sent = exchange(sent.reshape(experts, -1, LANES)).reshape(experts, cap, SUB, LANES)
        back = expert(sent, gate_k, gelu_k, gelu_slope_k, w_out_k, w_in_k, packed_k)
        back = exchange(back.reshape(experts, -1, LANES)).reshape(slots, SUB, LANES)
        kept = frame(taker, k % 2, lines, back, kept, arrived, normed_k, slope_k, packed_k)
        if k < sections - 1:
            arrived = lax.ppermute(kept, "section", [(sections - k, sections - 2 - k)])
            own_out = jnp.where(section == sections - 1 - k, kept, own_out)
            low_out = jnp.where(section == sections - k, kept, low_out)
    last = lax.ppermute(kept, "section", [(1, 0)])
    fetched = lax.ppermute(low_out, "section", [(i, i - 1) for i in range(2, sections)])
    rest = jnp.where(section == sections - 1, first[1], fetched)
    return finish(jnp.stack([odd, section]), own_out, kept, rest, last)[None]


def solution(mesh):
    in_specs = (
        P("section", None, "expert", None),
        P(None, "expert", None),
        P(None, "expert"),
        P("section", None, "expert"),
        P("section", None, "expert"),
        P("section", None, "expert", None),
        P("section", None, None),
        P("section", None),
        P("section", None, None),
        P("section", "expert", None, None),
        P("section", "expert", None, None),
    )
    out_specs = P("section", None, "expert", None)

    return jax.shard_map(
        on_device, mesh=mesh, in_specs=in_specs, out_specs=out_specs, check_vma=False
    )
```
